32 devices in a mesh: rows: 16 (over z, y, core), cols: 2 (over x).
Axes of the slice: x: 2, y: 2, z: 4, core: 2. Of those that a mesh axis runs over, the one named last changes fastest.
Arguments:
- matrix: float32 [8192, 8192], P('rows', 'cols'), may hold values from -6 to 6
- starts: int32 [4, 4], replicated, may hold values from 0 to 7936, as said below
- factors: float32 [4, 4, 256, 256], P(None, None, 'rows', 'cols'), as said below
Outputs:
- updated: float32 [8192, 8192], P('rows', 'cols')
The draws below stay inside these ranges and needn't reach their ends.
Inputs may be any that keep to these rules, and one draw needn't show every extreme that they name: `starts`: every start is a multiple of 128; chain c's start lies in the c-th of 4 equal ranges of blocks and never decreases from advance to advance; a window may end on the first block of the next range; the windows of one advance are disjoint. `factors`: every factor is orthogonal.
All inputs are finite; a program needn't handle non-finite values.
Results may differ from the reference program's by a relative error of at most 0.0001.
Values sent between devices are 32-bit elements; how exact they have to be, the bound alone decides.
A program may use at most 128 MiB of HBM per device.

```python
import jax
import jax.numpy as jnp
from jax import lax

N = 8192
NB = 128
CHAINS = 4
ADV = 4
W = 256
N_ROWS = 16
N_COLS = 2


def draw_starts(key, part):
    region = N // NB // CHAINS
    first_row = jnp.zeros((1, CHAINS), jnp.int32)
    middle_rows = jax.random.randint(jax.random.fold_in(key, 11), (ADV - 2, CHAINS), 1, region - 1)
    middle_rows = jnp.sort(middle_rows, axis=0).astype(jnp.int32)
    chain_ids = jnp.arange(CHAINS, dtype=jnp.int32)
    last_row = jnp.where(chain_ids == CHAINS - 1, region - 2, region - 1).astype(jnp.int32)[None, :]
    offsets = jnp.concatenate([first_row, middle_rows, last_row], axis=0)
    bases = chain_ids * region
    return ((bases[None, :] + offsets) * NB).astype(jnp.int32)


def draw_factors(key, part):
    gauss_draw = jax.random.normal(jax.random.fold_in(key, 23), (ADV, CHAINS, W, W), jnp.float32)
    orthog, upper = jnp.linalg.qr(gauss_draw)
    signs = jnp.where(jnp.diagonal(upper, axis1=-2, axis2=-1) >= 0.0, 1.0, -1.0)
    return (orthog * signs[..., None, :]).astype(jnp.float32)


def levels(own_key, dims, cuts, least, largest):
    level = 1.0
    for position, shards_of in cuts:
        steps = jax.random.uniform(jax.random.fold_in(jax.random.fold_in(own_key, 6), position), (shards_of,), jnp.float32, least / len(cuts), largest / len(cuts))
        level = level * jnp.repeat(jnp.exp(steps), dims[position] // shards_of).reshape((-1,) + (1,) * (len(dims) - 1 - position))
    return level


def gaussian(rng, shape, spread, limit, cuts=(), held_as=jnp.bfloat16):
    drawn = jax.random.normal(rng, shape, jnp.float32) * spread
    if len(cuts) > 0:
        drawn = levels(rng, shape, cuts, -0.22, 0.18) * drawn
    return jnp.clip(drawn, min=-limit, max=limit).astype(held_as)


def setup_inputs(seed: int = 0) -> dict:
    streams_of = jax.random.split(jax.random.key(seed), 4)
    matrix = gaussian(streams_of[0], (N, N), 1.0, 6.0, ((0, 16), (1, 2)), jnp.float32)
    starts = draw_starts(jax.random.fold_in(streams_of[3], 71), 0)
    factors = draw_factors(jax.random.fold_in(streams_of[3], 71), 0)
    return {"matrix": matrix, "starts": starts, "factors": factors}


def to_natural(source):
    rows_per = N // (N_ROWS * NB)
    cols_per = N // (N_COLS * NB)
    source = source.reshape(N_ROWS, rows_per, NB, N).transpose(1, 0, 2, 3).reshape(N, N)
    return source.reshape(N, N_COLS, cols_per, NB).transpose(0, 2, 1, 3).reshape(N, N)

def to_stored(source):
    rows_per = N // (N_ROWS * NB)
    cols_per = N // (N_COLS * NB)
    source = source.reshape(rows_per, N_ROWS, NB, N).transpose(1, 0, 2, 3).reshape(N, N)
    return source.reshape(N, cols_per, N_COLS, NB).transpose(0, 2, 1, 3).reshape(N, N)

def reference(matrix, starts, factors):
    active = to_natural(matrix)
    for advance in range(ADV):
        for chain_id in range(CHAINS):
            offset = starts[advance, chain_id].astype(jnp.int32)
            factor = factors[advance, chain_id]
            window_rows = lax.dynamic_slice_in_dim(active, offset, W, 0)
            changed = jnp.dot(factor.T.astype(jnp.float32), window_rows.astype(jnp.float32), precision=lax.Precision.HIGHEST, preferred_element_type=jnp.float32)
            active = lax.dynamic_update_slice_in_dim(active, changed, offset, 0)
        for chain_id in range(CHAINS):
            offset = starts[advance, chain_id].astype(jnp.int32)
            factor = factors[advance, chain_id]
            window_cols = lax.dynamic_slice_in_dim(active, offset, W, 1)
            changed = jnp.dot(window_cols.astype(jnp.float32), factor.astype(jnp.float32), precision=lax.Precision.HIGHEST, preferred_element_type=jnp.float32)
            active = lax.dynamic_update_slice_in_dim(active, changed, offset, 1)
    return to_stored(active)
```

```python
import functools

import jax
import jax.numpy as jnp
from jax import lax
from jax.experimental import pallas as pl
from jax.experimental.pallas import tpu as pltpu
from jax.sharding import PartitionSpec as P

NB = 128
VMEM_LIMIT = 60 * 1024 * 1024


def split(value):
    high = value.astype(jnp.bfloat16)
    low = (value - high.astype(jnp.float32)).astype(jnp.bfloat16)
    return high, low


def product(left, right, dims):
    lh, ll = split(left)
    rh, rl = split(right)
    dot = functools.partial(
        lax.dot_general, dimension_numbers=(dims, ((), ())), preferred_element_type=jnp.float32
    )
    return dot(lh, rh) + (dot(lh, rl) + dot(ll, rh))


def pack_kernel(slots, tile_ref, out_ref):
    out_ref[0] = tile_ref[...]


def pack_columns(tile, slots):
    rows = tile.shape[0]
    count = slots.shape[0]
    return pl.pallas_call(
        pack_kernel,
        out_shape=jax.ShapeDtypeStruct((count, rows, NB), tile.dtype),
        grid_spec=pltpu.PrefetchScalarGridSpec(
            num_scalar_prefetch=1,
            grid=(count,),
            in_specs=[pl.BlockSpec((rows, NB), lambda w, slots: (0, slots[w]))],
            out_specs=pl.BlockSpec((1, rows, NB), lambda w, slots: (w, 0, 0)),
        ),
        name="pack_columns",
    )(slots, tile)


def column_kernel(slots, ghosts, heads, tile_ref, ghost_ref, factor_ref, out_ref, held):
    out_ref[...] = tile_ref[...]
    held[...] = ghost_ref[...]

    def step(w, carry):
        at = pl.multiple_of(slots[w] * NB, NB)
        ghost = ghosts[w]
        head = heads[w]
        own_rows = pl.multiple_of((1 - head) * NB, NB)
        other_rows = pl.multiple_of(head * NB, NB)
        window = jnp.concatenate([out_ref[:, pl.ds(at, NB)], held[ghost]], axis=1)
        factor = jnp.concatenate(
            [factor_ref[w, pl.ds(own_rows, NB), :], factor_ref[w, pl.ds(other_rows, NB), :]], axis=0
        )
        turned = product(window, factor, ((1,), (0,)))
        first, second = turned[:, :NB], turned[:, NB:]
        is_head = head == 1
        out_ref[:, pl.ds(at, NB)] = jnp.where(is_head, first, second)
        held[ghost] = jnp.where(is_head, second, first)
        return carry

    lax.fori_loop(0, factor_ref.shape[0], step, 0)


def turn_columns(tile, ghost, factors, slots, ghosts, heads):
    rows, width = tile.shape
    count = ghost.shape[0]
    chunk = rows // 2
    order = factors.shape[-1]
    return pl.pallas_call(
        column_kernel,
        out_shape=jax.ShapeDtypeStruct(tile.shape, tile.dtype),
        grid_spec=pltpu.PrefetchScalarGridSpec(
            num_scalar_prefetch=3,
            grid=(rows // chunk,),
            in_specs=[
                pl.BlockSpec((chunk, width), lambda i, *_: (i, 0)),
                pl.BlockSpec((count, chunk, NB), lambda i, *_: (0, i, 0)),
                pl.BlockSpec((count, order, order), lambda i, *_: (0, 0, 0)),
            ],
            out_specs=pl.BlockSpec((chunk, width), lambda i, *_: (i, 0)),
            scratch_shapes=[pltpu.VMEM((count, chunk, NB), tile.dtype)],
        ),
        compiler_params=pltpu.CompilerParams(vmem_limit_bytes=VMEM_LIMIT),
        name="turn_columns",
    )(slots, ghosts, heads, tile, ghost, factors)


def columns_of_two(tile, blocks, whole_factors):
    position = lax.axis_index("cols")
    heads = (blocks % 2 == position).astype(jnp.int32)
    own = blocks + 1 - heads
    other = blocks + heads
    slots = own // 2
    same = other[:, None] == other[None, :]
    ghosts = jnp.argmax(same, axis=1).astype(jnp.int32)
    packed = pack_columns(tile, slots)
    ghost = lax.ppermute(packed, "cols", [(0, 1), (1, 0)])
    return turn_columns(tile, ghost, whole_factors, slots, ghosts, heads)


def from_behind(value, axis, steps):
    count = lax.axis_size(axis)
    pairs = [(source, (source + steps) % count) for source in range(count)]
    return lax.ppermute(value, axis, pairs)


def columns_of_many(tile, blocks, whole_factors, chains):
    position = lax.axis_index("cols")
    devices = lax.axis_size("cols")

    def owned(ids):
        parts, places = [], []
        for block in ids:
            start = block // devices * NB
            mine = block % devices == position
            part = lax.dynamic_slice_in_dim(tile, start, NB, 1)
            parts.append(jnp.where(mine, part, jnp.zeros_like(part)))
            places.append((start, mine))
        return jnp.stack(parts), places

    for first in range(0, blocks.shape[0], chains):
        ids = [blocks[first + c] for c in range(chains)]
        left, left_places = owned(ids)
        right, right_places = owned([block + 1 for block in ids])
        window = jnp.concatenate(
            [left + from_behind(left, "cols", 1), right + from_behind(right, "cols", -1)], axis=2
        )
        turned = jnp.einsum(
            "crj,cji->cri",
            window,
            whole_factors[first : first + chains],
            precision=lax.Precision.HIGHEST,
            preferred_element_type=jnp.float32,
        )
        for c in range(chains):
            for (start, mine), new in (
                (left_places[c], turned[c, :, :NB]),
                (right_places[c], turned[c, :, NB:]),
            ):
                now = lax.dynamic_slice_in_dim(tile, start, NB, 1)
                tile = lax.dynamic_update_slice_in_dim(tile, jnp.where(mine, new, now), start, 1)
    return tile


def plan_kernel(devices, count, blocks, me_ref, plan):
    me = me_ref[0]
    for t in range(count):
        plan[0, t] = -1
        plan[1, t] = -1
        plan[2, t] = 0
        plan[3, t] = 0
    block = [blocks[w] for w in range(count)]
    owner = [lax.rem(b, devices) for b in block]
    when = []
    for w in range(count):
        step = jnp.int32(0)
        for v in range(w):
            clash = (
                (block[w] == block[v])
                | (block[w] == block[v] + 1)
                | (block[w] + 1 == block[v])
                | (owner[w] == owner[v])
            )
            step = jnp.maximum(step, jnp.where(clash, when[v] + 1, 0))
        when.append(step)
        kind = jnp.where(
            lax.rem(owner[w], 2) == 0, 1, jnp.where(lax.rem(owner[w], 4) == 1, 2, 4)
        )
        plan[2, step] = plan[2, step] | kind
        plan[3, 0] = jnp.maximum(plan[3, 0], step + 1)
        after = lax.rem(owner[w] + 1, devices)

        @pl.when((owner[w] == me) | (after == me))
        def _():
            port = lax.rem(owner[w], 2)
            plan[port, step] = w


def make_plan(blocks, me, devices):
    count = blocks.shape[0]
    smem = pl.BlockSpec(memory_space=pltpu.SMEM)
    return pl.pallas_call(
        functools.partial(plan_kernel, devices, count),
        out_shape=jax.ShapeDtypeStruct((4, count), jnp.int32),
        in_specs=[smem, smem],
        out_specs=smem,
        name="plan_steps",
    )(blocks, me.reshape(1))


def row_kernel(meta, tile_ref, even_ref, odd_ref, factor_ref, out_ref):
    port = pl.program_id(0)
    valid = meta[port, 1]
    head = meta[port, 2]

    @pl.when(valid == 0)
    def _():
        out_ref[...] = tile_ref[...]

    @pl.when(valid == 1)
    def _():
        half = pl.multiple_of((1 - head) * NB, NB)
        other = pl.multiple_of(head * NB, NB)
        factor = jnp.concatenate(
            [
                factor_ref[0, pl.ds(half, NB), pl.ds(half, NB)],
                factor_ref[0, pl.ds(other, NB), pl.ds(half, NB)],
            ],
            axis=0,
        )
        ghost = jnp.where(port == 0, even_ref[...], odd_ref[...])
        window = jnp.concatenate([tile_ref[...], ghost], axis=0)
        out_ref[...] = product(factor.T, window, ((1,), (0,)))


def turn_rows(tile, even, odd, factors, meta):
    width = tile.shape[1]
    order = factors.shape[-1]
    pieces = 4 if width % (4 * NB) == 0 else 1
    chunk = width // pieces
    last = pieces - 1
    return pl.pallas_call(
        row_kernel,
        out_shape=jax.ShapeDtypeStruct(tile.shape, tile.dtype),
        grid_spec=pltpu.PrefetchScalarGridSpec(
            num_scalar_prefetch=1,
            grid=(2, pieces),
            in_specs=[
                pl.BlockSpec((NB, chunk), lambda p, j, meta: (meta[p, 0], j)),
                pl.BlockSpec((NB, chunk), lambda p, j, meta: (0, jnp.where(p == 0, j, last))),
                pl.BlockSpec((NB, chunk), lambda p, j, meta: (0, jnp.where(p == 1, j, 0))),
                pl.BlockSpec((1, order, order), lambda p, j, meta: (meta[p, 3], 0, 0)),
            ],
            out_specs=pl.BlockSpec((NB, chunk), lambda p, j, meta: (meta[p, 0], j)),
        ),
        input_output_aliases={1: 0},
        compiler_params=pltpu.CompilerParams(vmem_limit_bytes=VMEM_LIMIT),
        name="turn_rows",
    )(meta, tile, even, odd, factors)


def turn_all_rows(tile, blocks, whole_factors):
    me = lax.axis_index("rows")
    devices = lax.axis_size("rows")
    slots = tile.shape[0] // NB
    plan = make_plan(blocks, me, devices)

    def pairs(lows):
        ways = []
        for low in lows:
            high = (low + 1) % devices
            ways += [(low, high), (high, low)]
        return ways

    even_ways = pairs(range(0, devices, 2))
    odd_ways = {
        2: pairs(range(1, devices, 4)),
        4: pairs(range(3, devices, 4)),
        6: pairs(range(1, devices, 2)),
    }

    def exchange(kinds, even, odd):
        if kinds & 1:
            even = lax.ppermute(even, "rows", even_ways)
        if kinds & 6:
            odd = lax.ppermute(odd, "rows", odd_ways[kinds & 6])
        return even, odd

    branches = [functools.partial(exchange, kinds) for kinds in range(8)]

    def step(t, tile):
        windows = plan[:2, t]
        valid = windows >= 0
        chosen = jnp.maximum(windows, 0)
        block = blocks[chosen]
        head = block % devices == me
        slot = jnp.where(valid, (block + 1 - head) // devices, 0)
        spare = (slot[::-1] + 1) % slots
        slot = jnp.where(valid | (~valid[::-1] & (jnp.arange(2) == 0)), slot, spare)
        meta = jnp.stack(
            [slot, valid.astype(jnp.int32), head.astype(jnp.int32), chosen], axis=1
        ).astype(jnp.int32)
        even = lax.dynamic_slice_in_dim(tile, slot[0] * NB, NB, 0)
        odd = lax.dynamic_slice_in_dim(tile, slot[1] * NB, NB, 0)
        even, odd = lax.switch(plan[2, t], branches, even, odd)
        return turn_rows(tile, even, odd, whole_factors, meta)

    return lax.fori_loop(0, plan[3, 0], step, tile)


def local(matrix, starts, factors):
    advances, chains = starts.shape
    blocks = (starts // NB).reshape(advances * chains)
    whole = lax.all_gather(factors, "rows", axis=2, tiled=True)
    whole = lax.all_gather(whole, "cols", axis=3, tiled=True)
    whole = whole.reshape((advances * chains,) + whole.shape[2:])
    if lax.axis_size("cols") == 2:
        tile = columns_of_two(matrix, blocks, whole)
    else:
        tile = columns_of_many(matrix, blocks, whole, chains)
    return turn_all_rows(tile, blocks, whole)


def solution(mesh):
    return jax.shard_map(
        local,
        mesh=mesh,
        in_specs=(P("rows", "cols"), P(), P(None, None, "rows", "cols")),
        out_specs=P("rows", "cols"),
        check_vma=False,
    )
```

```python
import functools

import jax
import jax.numpy as jnp
from jax import lax
from jax.experimental import pallas as pl
from jax.experimental.pallas import tpu as pltpu
from jax.sharding import PartitionSpec as P

NB = 128
VMEM_LIMIT = 60 * 1024 * 1024


def split(value):
    high = value.astype(jnp.bfloat16)
    low = (value - high.astype(jnp.float32)).astype(jnp.bfloat16)
    return high, low


def product(left, right, dims):
    lh, ll = split(left)
    rh, rl = split(right)
    dot = functools.partial(
        lax.dot_general, dimension_numbers=(dims, ((), ())), preferred_element_type=jnp.float32
    )
    return dot(lh, rh) + (dot(lh, rl) + dot(ll, rh))


def pack_kernel(slots, tile_ref, out_ref):
    out_ref[0] = tile_ref[...]


def pack_columns(tile, slots):
    rows = tile.shape[0]
    count = slots.shape[0]
    return pl.pallas_call(
        pack_kernel,
        out_shape=jax.ShapeDtypeStruct((count, rows, NB), tile.dtype),
        grid_spec=pltpu.PrefetchScalarGridSpec(
            num_scalar_prefetch=1,
            grid=(count,),
            in_specs=[pl.BlockSpec((rows, NB), lambda w, slots: (0, slots[w]))],
            out_specs=pl.BlockSpec((1, rows, NB), lambda w, slots: (w, 0, 0)),
        ),
        name="pack_columns",
    )(slots, tile)


def column_kernel(slots, ghosts, heads, tile_ref, ghost_ref, factor_ref, out_ref, held):
    out_ref[...] = tile_ref[...]
    held[...] = ghost_ref[...]

    def step(w, carry):
        at = pl.multiple_of(slots[w] * NB, NB)
        ghost = ghosts[w]
        head = heads[w]
        own_rows = pl.multiple_of((1 - head) * NB, NB)
        other_rows = pl.multiple_of(head * NB, NB)
        window = jnp.concatenate([out_ref[:, pl.ds(at, NB)], held[ghost]], axis=1)
        factor = jnp.concatenate(
            [factor_ref[w, pl.ds(own_rows, NB), :], factor_ref[w, pl.ds(other_rows, NB), :]], axis=0
        )
        turned = product(window, factor, ((1,), (0,)))
        first, second = turned[:, :NB], turned[:, NB:]
        is_head = head == 1
        out_ref[:, pl.ds(at, NB)] = jnp.where(is_head, first, second)
        held[ghost] = jnp.where(is_head, second, first)
        return carry

    lax.fori_loop(0, factor_ref.shape[0], step, 0)


def turn_columns(tile, ghost, factors, slots, ghosts, heads):
    rows, width = tile.shape
    count = ghost.shape[0]
    chunk = rows // 2
    order = factors.shape[-1]
    return pl.pallas_call(
        column_kernel,
        out_shape=jax.ShapeDtypeStruct(tile.shape, tile.dtype),
        grid_spec=pltpu.PrefetchScalarGridSpec(
            num_scalar_prefetch=3,
            grid=(rows // chunk,),
            in_specs=[
                pl.BlockSpec((chunk, width), lambda i, *_: (i, 0)),
                pl.BlockSpec((count, chunk, NB), lambda i, *_: (0, i, 0)),
                pl.BlockSpec((count, order, order), lambda i, *_: (0, 0, 0)),
            ],
            out_specs=pl.BlockSpec((chunk, width), lambda i, *_: (i, 0)),
            scratch_shapes=[pltpu.VMEM((count, chunk, NB), tile.dtype)],
        ),
        compiler_params=pltpu.CompilerParams(vmem_limit_bytes=VMEM_LIMIT),
        name="turn_columns",
    )(slots, ghosts, heads, tile, ghost, factors)


def columns_of_two(tile, blocks, whole_factors):
    position = lax.axis_index("cols")
    heads = (blocks % 2 == position).astype(jnp.int32)
    own = blocks + 1 - heads
    other = blocks + heads
    slots = own // 2
    same = other[:, None] == other[None, :]
    ghosts = jnp.argmax(same, axis=1).astype(jnp.int32)
    packed = pack_columns(tile, slots)
    ghost = lax.ppermute(packed, "cols", [(0, 1), (1, 0)])
    return turn_columns(tile, ghost, whole_factors, slots, ghosts, heads)


def from_behind(value, axis, steps):
    count = lax.axis_size(axis)
    pairs = [(source, (source + steps) % count) for source in range(count)]
    return lax.ppermute(value, axis, pairs)


def columns_of_many(tile, blocks, whole_factors, chains):
    position = lax.axis_index("cols")
    devices = lax.axis_size("cols")

    def owned(ids):
        parts, places = [], []
        for block in ids:
            start = block // devices * NB
            mine = block % devices == position
            part = lax.dynamic_slice_in_dim(tile, start, NB, 1)
            parts.append(jnp.where(mine, part, jnp.zeros_like(part)))
            places.append((start, mine))
        return jnp.stack(parts), places

    for first in range(0, blocks.shape[0], chains):
        ids = [blocks[first + c] for c in range(chains)]
        left, left_places = owned(ids)
        right, right_places = owned([block + 1 for block in ids])
        window = jnp.concatenate(
            [left + from_behind(left, "cols", 1), right + from_behind(right, "cols", -1)], axis=2
        )
        turned = jnp.einsum(
            "crj,cji->cri",
            window,
            whole_factors[first : first + chains],
            precision=lax.Precision.HIGHEST,
            preferred_element_type=jnp.float32,
        )
        for c in range(chains):
            for (start, mine), new in (
                (left_places[c], turned[c, :, :NB]),
                (right_places[c], turned[c, :, NB:]),
            ):
                now = lax.dynamic_slice_in_dim(tile, start, NB, 1)
                tile = lax.dynamic_update_slice_in_dim(tile, jnp.where(mine, new, now), start, 1)
    return tile


def plan_kernel(devices, slots, count, blocks, me_ref, plan):
    me = me_ref[0]

    def clear(t, carry):
        for row in range(slots + 1):
            plan[row, t] = -1
        for row in range(slots + 1, slots + 4):
            plan[row, t] = 0
        return carry

    lax.fori_loop(0, count, clear, 0)
    block = [blocks[w] for w in range(count)]
    owner = [lax.rem(b, devices) for b in block]
    when = []
    for w in range(count):
        step = jnp.int32(0)
        odd = lax.rem(owner[w], 2)
        for v in range(w):
            clash = (
                (block[w] == block[v])
                | (block[w] == block[v] + 1)
                | (block[w] + 1 == block[v])
                | ((owner[w] == owner[v]) & (odd == 1))
            )
            step = jnp.maximum(step, jnp.where(clash, when[v] + 1, 0))
        when.append(step)
        kind = jnp.where(odd == 0, 1, jnp.where(lax.rem(owner[w], 4) == 1, 2, 4))
        plan[slots + 2, step] = plan[slots + 2, step] | kind
        plan[slots + 3, 0] = jnp.maximum(plan[slots + 3, 0], step + 1)
        is_head = owner[w] == me

        @pl.when(is_head | (lax.rem(owner[w] + 1, devices) == me))
        def _():
            slot = jnp.where(is_head, block[w], block[w] + 1) // devices
            row = jnp.where(odd == 1, slots, slot)
            plan[row, step] = 2 * w + is_head.astype(jnp.int32)
            plan[slots + 1, step] = jnp.where(odd == 1, slot, plan[slots + 1, step])


def make_plan(blocks, me, devices, slots):
    count = blocks.shape[0]
    smem = pl.BlockSpec(memory_space=pltpu.SMEM)
    return pl.pallas_call(
        functools.partial(plan_kernel, devices, slots, count),
        out_shape=jax.ShapeDtypeStruct((slots + 4, count), jnp.int32),
        in_specs=[smem, smem],
        out_specs=smem,
        name="plan_steps",
    )(blocks, me.reshape(1))


def row_kernel(
    slots, pieces, plan, t_ref, tile, even, odd, factors, out,
    mine, ghost, factor, mine_sem, ghost_sem, factor_sem, out_sem,
):
    t = t_ref[0]
    width = mine.shape[2]
    chunk = width // pieces
    jobs = slots + 1

    def place(job):
        slot = job if job < slots else plan[slots + 1, t]
        return pl.ds(pl.multiple_of(slot * NB, NB), NB)

    def loads(job):
        code = jnp.maximum(plan[job, t], 0)
        source = even.at[pl.ds(job * NB, NB), :] if job < slots else odd
        return (
            pltpu.make_async_copy(tile.at[place(job), :], mine.at[job], mine_sem.at[job]),
            pltpu.make_async_copy(source, ghost.at[job], ghost_sem.at[job]),
            pltpu.make_async_copy(factors.at[code // 2], factor.at[job], factor_sem.at[job]),
        )

    def store(job):
        return pltpu.make_async_copy(mine.at[job], out.at[place(job), :], out_sem.at[job])

    for job in range(jobs):

        @pl.when(plan[job, t] >= 0)
        def _():
            for copy in loads(job):
                copy.start()

    for job in range(jobs):

        @pl.when(plan[job, t] >= 0)
        def _():
            for copy in loads(job):
                copy.wait()
            head = lax.rem(plan[job, t], 2)
            near = pl.multiple_of((1 - head) * NB, NB)
            far = pl.multiple_of(head * NB, NB)
            turn = jnp.concatenate(
                [factor[job, pl.ds(near, NB), pl.ds(near, NB)], factor[job, pl.ds(far, NB), pl.ds(near, NB)]],
                axis=0,
            ).T

            def piece(j, carry):
                at = pl.ds(pl.multiple_of(j * chunk, NB), chunk)
                window = jnp.concatenate([mine[job, :, at], ghost[job, :, at]], axis=0)
                mine[job, :, at] = product(turn, window, ((1,), (0,)))
                return carry

            lax.fori_loop(0, pieces, piece, 0)
            store(job).start()

    for job in range(jobs):

        @pl.when(plan[job, t] >= 0)
        def _():
            store(job).wait()


def turn_rows(plan, t, tile, even, odd, factors):
    width = tile.shape[1]
    slots = tile.shape[0] // NB
    jobs = slots + 1
    order = factors.shape[-1]
    pieces = 4 if width % (4 * NB) == 0 else 1
    smem = pl.BlockSpec(memory_space=pltpu.SMEM)
    any_space = pl.BlockSpec(memory_space=pl.ANY)
    return pl.pallas_call(
        functools.partial(row_kernel, slots, pieces),
        out_shape=jax.ShapeDtypeStruct(tile.shape, tile.dtype),
        in_specs=[smem, smem] + [any_space] * 4,
        out_specs=any_space,
        scratch_shapes=[
            pltpu.VMEM((jobs, NB, width), tile.dtype),
            pltpu.VMEM((jobs, NB, width), tile.dtype),
            pltpu.VMEM((jobs, order, order), tile.dtype),
        ]
        + [pltpu.SemaphoreType.DMA((jobs,))] * 4,
        input_output_aliases={2: 0},
        compiler_params=pltpu.CompilerParams(vmem_limit_bytes=VMEM_LIMIT),
        name="turn_rows",
    )(plan, t.reshape(1), tile, even, odd, factors)


def unset(shape, dtype):
    return pl.pallas_call(
        lambda out: None,
        out_shape=jax.ShapeDtypeStruct(shape, dtype),
        out_specs=pl.BlockSpec(memory_space=pl.ANY),
        name="unset",
    )()


def turn_all_rows(tile, blocks, whole_factors):
    me = lax.axis_index("rows")
    devices = lax.axis_size("rows")
    slots = tile.shape[0] // NB
    plan = make_plan(blocks, me, devices, slots)

    def pairs(lows):
        ways = []
        for low in lows:
            high = (low + 1) % devices
            ways += [(low, high), (high, low)]
        return ways

    even_ways = pairs(range(0, devices, 2))
    odd_ways = {
        2: pairs(range(1, devices, 4)),
        4: pairs(range(3, devices, 4)),
        6: pairs(range(1, devices, 2)),
    }

    def exchange(kinds, tile, odd):
        even = unset(tile.shape, tile.dtype)
        far = unset(odd.shape, odd.dtype)
        if kinds & 1:
            even = lax.ppermute(tile, "rows", even_ways)
        if kinds & 6:
            far = lax.ppermute(odd, "rows", odd_ways[kinds & 6])
        return even, far

    branches = [functools.partial(exchange, kinds) for kinds in range(8)]

    def step(t, tile):
        odd = lax.dynamic_slice_in_dim(tile, plan[slots + 1, t] * NB, NB, 0)
        even, odd = lax.switch(plan[slots + 2, t], branches, tile, odd)
        return turn_rows(plan, t, tile, even, odd, whole_factors)

    return lax.fori_loop(0, plan[slots + 3, 0], step, tile)


def local(matrix, starts, factors):
    advances, chains = starts.shape
    blocks = (starts // NB).reshape(advances * chains)
    whole = lax.all_gather(factors, "cols", axis=3, tiled=True)
    whole = lax.all_gather(whole, "rows", axis=2, tiled=True)
    whole = whole.reshape((advances * chains,) + whole.shape[2:])
    if lax.axis_size("cols") == 2:
        tile = columns_of_two(matrix, blocks, whole)
    else:
        tile = columns_of_many(matrix, blocks, whole, chains)
    return turn_all_rows(tile, blocks, whole)


def solution(mesh):
    return jax.shard_map(
        local,
        mesh=mesh,
        in_specs=(P("rows", "cols"), P(), P(None, None, "rows", "cols")),
        out_specs=P("rows", "cols"),
        check_vma=False,
    )
```

```python
import functools

import jax
import jax.numpy as jnp
from jax import lax
from jax.experimental import pallas as pl
from jax.experimental.pallas import tpu as pltpu
from jax.sharding import PartitionSpec as P

NB = 128
VMEM_LIMIT = 60 * 1024 * 1024


def split(value):
    high = value.astype(jnp.bfloat16)
    low = (value - high.astype(jnp.float32)).astype(jnp.bfloat16)
    return high, low


def product(left, right, dims):
    lh, ll = split(left)
    rh, rl = split(right)
    dot = functools.partial(
        lax.dot_general, dimension_numbers=(dims, ((), ())), preferred_element_type=jnp.float32
    )
    return dot(lh, rh) + (dot(lh, rl) + dot(ll, rh))


def pack_kernel(slots, tile_ref, out_ref):
    out_ref[0] = tile_ref[...]


def pack_columns(tile, slots, part, parts):
    rows = tile.shape[0] // parts
    count = slots.shape[0]
    return pl.pallas_call(
        pack_kernel,
        out_shape=jax.ShapeDtypeStruct((count, rows, NB), tile.dtype),
        grid_spec=pltpu.PrefetchScalarGridSpec(
            num_scalar_prefetch=1,
            grid=(count,),
            in_specs=[pl.BlockSpec((rows, NB), lambda w, slots: (part, slots[w]))],
            out_specs=pl.BlockSpec((1, rows, NB), lambda w, slots: (w, 0, 0)),
        ),
        cost_estimate=pl.CostEstimate(
            flops=0, transcendentals=0, bytes_accessed=8 * count * rows * NB
        ),
        name="pack_columns",
    )(slots, tile)


def column_kernel(slots, ghosts, heads, tile_ref, ghost_ref, factor_ref, out_ref, held):
    out_ref[...] = tile_ref[...]
    held[...] = ghost_ref[...]

    def step(w, carry):
        at = pl.multiple_of(slots[w] * NB, NB)
        ghost = ghosts[w]
        head = heads[w]
        own_rows = pl.multiple_of((1 - head) * NB, NB)
        other_rows = pl.multiple_of(head * NB, NB)
        window = jnp.concatenate([out_ref[:, pl.ds(at, NB)], held[ghost]], axis=1)
        factor = jnp.concatenate(
            [factor_ref[w, pl.ds(own_rows, NB), :], factor_ref[w, pl.ds(other_rows, NB), :]], axis=0
        )
        turned = product(window, factor, ((1,), (0,)))
        first, second = turned[:, :NB], turned[:, NB:]
        is_head = head == 1
        out_ref[:, pl.ds(at, NB)] = jnp.where(is_head, first, second)
        held[ghost] = jnp.where(is_head, second, first)
        return carry

    lax.fori_loop(0, factor_ref.shape[0], step, 0)


def turn_columns(tile, ghost, factors, slots, ghosts, heads, part):
    width = tile.shape[1]
    count, rows, _ = ghost.shape
    order = factors.shape[-1]
    return pl.pallas_call(
        column_kernel,
        out_shape=jax.ShapeDtypeStruct((rows, width), tile.dtype),
        grid_spec=pltpu.PrefetchScalarGridSpec(
            num_scalar_prefetch=3,
            grid=(1,),
            in_specs=[
                pl.BlockSpec((rows, width), lambda i, *_: (part, 0)),
                pl.BlockSpec((count, rows, NB), lambda i, *_: (0, 0, 0)),
                pl.BlockSpec((count, order, order), lambda i, *_: (0, 0, 0)),
            ],
            out_specs=pl.BlockSpec((rows, width), lambda i, *_: (0, 0)),
            scratch_shapes=[pltpu.VMEM((count, rows, NB), tile.dtype)],
        ),
        compiler_params=pltpu.CompilerParams(vmem_limit_bytes=VMEM_LIMIT),
        cost_estimate=pl.CostEstimate(
            flops=6 * count * rows * order * order,
            transcendentals=0,
            bytes_accessed=4 * (2 * rows * width + count * rows * NB + count * order * order),
        ),
        name="turn_columns",
    )(slots, ghosts, heads, tile, ghost, factors)


def exchange_columns(tile, blocks, parts):
    position = lax.axis_index("cols")
    heads = (blocks % 2 == position).astype(jnp.int32)
    own = blocks + 1 - heads
    other = blocks + heads
    slots = own // 2
    same = other[:, None] == other[None, :]
    ghosts = jnp.argmax(same, axis=1).astype(jnp.int32)
    packed, came = [], []
    for part in range(parts):
        packed.append(pack_columns(tile, slots, part, parts))
        came.append(lax.ppermute(packed[part], "cols", [(0, 1), (1, 0)]))
    return packed, came, (slots, ghosts, heads)


def from_behind(value, axis, steps):
    count = lax.axis_size(axis)
    pairs = [(source, (source + steps) % count) for source in range(count)]
    return lax.ppermute(value, axis, pairs)


def columns_of_many(tile, blocks, whole_factors, chains):
    position = lax.axis_index("cols")
    devices = lax.axis_size("cols")

    def owned(ids):
        parts, places = [], []
        for block in ids:
            start = block // devices * NB
            mine = block % devices == position
            part = lax.dynamic_slice_in_dim(tile, start, NB, 1)
            parts.append(jnp.where(mine, part, jnp.zeros_like(part)))
            places.append((start, mine))
        return jnp.stack(parts), places

    for first in range(0, blocks.shape[0], chains):
        ids = [blocks[first + c] for c in range(chains)]
        left, left_places = owned(ids)
        right, right_places = owned([block + 1 for block in ids])
        window = jnp.concatenate(
            [left + from_behind(left, "cols", 1), right + from_behind(right, "cols", -1)], axis=2
        )
        turned = jnp.einsum(
            "crj,cji->cri",
            window,
            whole_factors[first : first + chains],
            precision=lax.Precision.HIGHEST,
            preferred_element_type=jnp.float32,
        )
        for c in range(chains):
            for (start, mine), new in (
                (left_places[c], turned[c, :, :NB]),
                (right_places[c], turned[c, :, NB:]),
            ):
                now = lax.dynamic_slice_in_dim(tile, start, NB, 1)
                tile = lax.dynamic_update_slice_in_dim(tile, jnp.where(mine, new, now), start, 1)
    return tile


def plan_kernel(devices, slots, count, blocks, me_ref, plan):
    me = me_ref[0]

    def clear(t, carry):
        for row in range(slots + 1):
            plan[row, t] = -1
        for row in range(slots + 1, slots + 4):
            plan[row, t] = 0
        return carry

    lax.fori_loop(0, count, clear, 0)
    block = [blocks[w] for w in range(count)]
    owner = [lax.rem(b, devices) for b in block]
    when = []
    for w in range(count):
        odd = lax.rem(owner[w], 2)
        step = odd
        for v in range(w):
            clash = (
                (block[w] == block[v])
                | (block[w] == block[v] + 1)
                | (block[w] + 1 == block[v])
                | ((owner[w] == owner[v]) & (odd == 1))
            )
            step = jnp.maximum(step, jnp.where(clash, when[v] + 1, 0))
        when.append(step)
        kind = jnp.where(odd == 0, 1, jnp.where(lax.rem(owner[w], 4) == 1, 2, 4))
        plan[slots + 2, step] = plan[slots + 2, step] | kind
        plan[slots + 3, 0] = jnp.maximum(plan[slots + 3, 0], step + 1)
        is_head = owner[w] == me

        @pl.when(is_head | (lax.rem(owner[w] + 1, devices) == me))
        def _():
            slot = jnp.where(is_head, block[w], block[w] + 1) // devices
            row = jnp.where(odd == 1, slots, slot)
            plan[row, step] = 2 * w + is_head.astype(jnp.int32)
            plan[slots + 1, step] = jnp.where(odd == 1, slot, plan[slots + 1, step])


def make_plan(blocks, me, devices, slots):
    count = blocks.shape[0]
    smem = pl.BlockSpec(memory_space=pltpu.SMEM)
    return pl.pallas_call(
        functools.partial(plan_kernel, devices, slots, count),
        out_shape=jax.ShapeDtypeStruct((slots + 4, count), jnp.int32),
        in_specs=[smem, smem],
        out_specs=smem,
        name="plan_steps",
    )(blocks, me.reshape(1))


def turn_block(code, job, mine, ghost, factor, pieces, chunk):
    head = lax.rem(code, 2)
    near = pl.multiple_of((1 - head) * NB, NB)
    far = pl.multiple_of(head * NB, NB)
    turn = jnp.concatenate(
        [
            factor[job, pl.ds(near, NB), pl.ds(near, NB)],
            factor[job, pl.ds(far, NB), pl.ds(near, NB)],
        ],
        axis=0,
    ).T

    def piece(j, carry):
        at = pl.ds(pl.multiple_of(j * chunk, NB), chunk)
        window = jnp.concatenate([mine[job, :, at], ghost[job, :, at]], axis=0)
        mine[job, :, at] = product(turn, window, ((1,), (0,)))
        return carry

    lax.fori_loop(0, pieces, piece, 0)


def row_kernel(
    slots, pieces, plan, t_ref, tile, even, odd, factors, out,
    mine, ghost, factor, mine_sem, ghost_sem, factor_sem, out_sem,
):
    t = t_ref[0]
    width = mine.shape[2]
    chunk = width // pieces
    jobs = slots + 1

    def place(job):
        slot = job if job < slots else plan[slots + 1, t]
        return pl.ds(pl.multiple_of(slot * NB, NB), NB)

    def loads(job):
        code = jnp.maximum(plan[job, t], 0)
        source = even.at[pl.ds(job * NB, NB), :] if job < slots else odd
        return (
            pltpu.make_async_copy(tile.at[place(job), :], mine.at[job], mine_sem.at[job]),
            pltpu.make_async_copy(source, ghost.at[job], ghost_sem.at[job]),
            pltpu.make_async_copy(factors.at[code // 2], factor.at[job], factor_sem.at[job]),
        )

    def store(job):
        return pltpu.make_async_copy(mine.at[job], out.at[place(job), :], out_sem.at[job])

    for job in range(jobs):

        @pl.when(plan[job, t] >= 0)
        def _():
            for copy in loads(job):
                copy.start()

    for job in range(jobs):

        @pl.when(plan[job, t] >= 0)
        def _():
            for copy in loads(job):
                copy.wait()
            turn_block(plan[job, t], job, mine, ghost, factor, pieces, chunk)
            store(job).start()

    for job in range(jobs):

        @pl.when(plan[job, t] >= 0)
        def _():
            store(job).wait()


def turn_rows(plan, t, tile, even, odd, factors):
    width = tile.shape[1]
    slots = tile.shape[0] // NB
    jobs = slots + 1
    order = factors.shape[-1]
    pieces = 4 if width % (4 * NB) == 0 else 1
    smem = pl.BlockSpec(memory_space=pltpu.SMEM)
    any_space = pl.BlockSpec(memory_space=pl.ANY)
    return pl.pallas_call(
        functools.partial(row_kernel, slots, pieces),
        out_shape=jax.ShapeDtypeStruct(tile.shape, tile.dtype),
        in_specs=[smem, smem] + [any_space] * 4,
        out_specs=any_space,
        scratch_shapes=[
            pltpu.VMEM((jobs, NB, width), tile.dtype),
            pltpu.VMEM((jobs, NB, width), tile.dtype),
            pltpu.VMEM((jobs, order, order), tile.dtype),
        ]
        + [pltpu.SemaphoreType.DMA((jobs,))] * 4,
        input_output_aliases={2: 0},
        compiler_params=pltpu.CompilerParams(vmem_limit_bytes=VMEM_LIMIT),
        name="turn_rows",
    )(plan, t.reshape(1), tile, even, odd, factors)


def even_kernel(base, pieces, plan, part, even, factors, *rest):
    out, mine, ghost, factor, mine_sem, ghost_sem, factor_sem, out_sem = rest[-8:]
    jobs, _, width = mine.shape
    chunk = width // pieces

    def load(job):
        return pltpu.make_async_copy(
            part.at[pl.ds(job * NB, NB), :], mine.at[job], mine_sem.at[job]
        )

    def others(job):
        code = jnp.maximum(plan[base + job, 0], 0)
        return (
            pltpu.make_async_copy(
                even.at[pl.ds(job * NB, NB), :], ghost.at[job], ghost_sem.at[job]
            ),
            pltpu.make_async_copy(factors.at[code // 2], factor.at[job], factor_sem.at[job]),
        )

    def store(job):
        return pltpu.make_async_copy(
            mine.at[job], out.at[pl.ds((base + job) * NB, NB), :], out_sem.at[job]
        )

    for job in range(jobs):
        load(job).start()

        @pl.when(plan[base + job, 0] >= 0)
        def _():
            for copy in others(job):
                copy.start()

    for job in range(jobs):
        load(job).wait()

        @pl.when(plan[base + job, 0] >= 0)
        def _():
            for copy in others(job):
                copy.wait()
            turn_block(plan[base + job, 0], job, mine, ghost, factor, pieces, chunk)

        store(job).start()
    for job in range(jobs):
        store(job).wait()


def turn_even(plan, part, even, factors, base, slots, tile=None):
    rows, width = part.shape
    jobs = rows // NB
    order = factors.shape[-1]
    pieces = 4 if width % (4 * NB) == 0 else 1
    any_space = pl.BlockSpec(memory_space=pl.ANY)
    extra = () if tile is None else (tile,)
    return pl.pallas_call(
        functools.partial(even_kernel, base, pieces),
        out_shape=jax.ShapeDtypeStruct((slots * NB, width), part.dtype),
        in_specs=[pl.BlockSpec(memory_space=pltpu.SMEM)] + [any_space] * (3 + len(extra)),
        out_specs=any_space,
        scratch_shapes=[
            pltpu.VMEM((jobs, NB, width), part.dtype),
            pltpu.VMEM((jobs, NB, width), part.dtype),
            pltpu.VMEM((jobs, order, order), part.dtype),
        ]
        + [pltpu.SemaphoreType.DMA((jobs,))] * 4,
        input_output_aliases={} if tile is None else {4: 0},
        compiler_params=pltpu.CompilerParams(vmem_limit_bytes=VMEM_LIMIT),
        cost_estimate=pl.CostEstimate(
            flops=6 * rows * 2 * NB * width, transcendentals=0, bytes_accessed=12 * rows * width
        ),
        name="turn_even",
    )(plan, part, even, factors, *extra)


def unset(shape, dtype):
    return pl.pallas_call(
        lambda out: None,
        out_shape=jax.ShapeDtypeStruct(shape, dtype),
        out_specs=pl.BlockSpec(memory_space=pl.ANY),
        name="unset",
    )()


def turn_all_rows(plan, column_parts, slots, whole_factors):
    devices = lax.axis_size("rows")

    def pairs(lows):
        ways = []
        for low in lows:
            high = (low + 1) % devices
            ways += [(low, high), (high, low)]
        return ways

    even_ways = pairs(range(0, devices, 2))
    odd_ways = {
        2: pairs(range(1, devices, 4)),
        4: pairs(range(3, devices, 4)),
        6: pairs(range(1, devices, 2)),
    }

    tile = None
    base = 0
    for column_part in column_parts:
        part, tile = column_part(tile)
        even = lax.ppermute(part, "rows", even_ways)
        tile = turn_even(plan, part, even, whole_factors, base, slots, tile)
        base += part.shape[0] // NB

    def exchange(kinds, tile, odd):
        even = unset(tile.shape, tile.dtype)
        far = unset(odd.shape, odd.dtype)
        if kinds & 1:
            even = lax.ppermute(tile, "rows", even_ways)
        if kinds & 6:
            far = lax.ppermute(odd, "rows", odd_ways[kinds & 6])
        return even, far

    branches = [functools.partial(exchange, kinds) for kinds in range(8)]

    def step(t, tile):
        odd = lax.dynamic_slice_in_dim(tile, plan[slots + 1, t] * NB, NB, 0)
        even, odd = lax.switch(plan[slots + 2, t], branches, tile, odd)
        return turn_rows(plan, t, tile, even, odd, whole_factors)

    return lax.fori_loop(1, plan[slots + 3, 0], step, tile)


def gather(factors, windows):
    if lax.axis_size("cols") == 2:
        other = lax.ppermute(factors, "cols", [(0, 1), (1, 0)])
        first = lax.axis_index("cols") == 0
        whole = jnp.concatenate(
            [jnp.where(first, factors, other), jnp.where(first, other, factors)], axis=3
        )
    else:
        whole = lax.all_gather(factors, "cols", axis=3, tiled=True)
    whole = lax.all_gather(whole, "rows", axis=2, tiled=True)
    return whole.reshape((windows,) + whole.shape[2:])


def local(matrix, starts, factors):
    advances, chains = starts.shape
    windows = advances * chains
    blocks = (starts // NB).reshape(windows)
    slots = matrix.shape[0] // NB
    parts = 2 if slots % 2 == 0 else 1
    plan = make_plan(blocks, lax.axis_index("rows"), lax.axis_size("rows"), slots)
    if lax.axis_size("cols") == 2:
        whole = gather(factors, windows)
        packed, came, tables = exchange_columns(matrix, blocks, parts)
        whole, plan, *_ = lax.optimization_barrier((whole, plan, *packed[1:]))

        def column_part(part, tile):
            ghost = came[part]
            if tile is not None:
                ghost, tile = lax.optimization_barrier((ghost, tile))
            return turn_columns(matrix, ghost, whole, *tables, part), tile

        column_parts = [functools.partial(column_part, part) for part in range(parts)]
    else:
        whole = gather(factors, windows)
        tile = columns_of_many(matrix, blocks, whole, chains)
        column_parts = [
            functools.partial(lambda piece, tile: (piece, tile), piece)
            for piece in jnp.split(tile, parts)
        ]
    return turn_all_rows(plan, column_parts, slots, whole)


def solution(mesh):
    return jax.shard_map(
        local,
        mesh=mesh,
        in_specs=(P("rows", "cols"), P(), P(None, None, "rows", "cols")),
        out_specs=P("rows", "cols"),
        check_vma=False,
    )
```

```python
import functools

import jax
import jax.numpy as jnp
from jax import lax
from jax.experimental import pallas as pl
from jax.experimental.pallas import tpu as pltpu
from jax.sharding import PartitionSpec as P

NB = 128
VMEM_LIMIT = 60 * 1024 * 1024


def split(value):
    high = value.astype(jnp.bfloat16)
    low = (value - high.astype(jnp.float32)).astype(jnp.bfloat16)
    return high, low


def product(left, right, dims):
    lh, ll = split(left)
    rh, rl = split(right)
    dot = functools.partial(
        lax.dot_general, dimension_numbers=(dims, ((), ())), preferred_element_type=jnp.float32
    )
    return dot(lh, rh) + (dot(lh, rl) + dot(ll, rh))


def pack_kernel(part, slots, tile, out, held, load_sem, store_sem):
    count, rows, _ = held.shape

    def load(w):
        at = pl.ds(pl.multiple_of(slots[w] * NB, NB), NB)
        return pltpu.make_async_copy(
            tile.at[pl.ds(part * rows, rows), at], held.at[w], load_sem.at[w]
        )

    def store(w):
        return pltpu.make_async_copy(held.at[w], out.at[w], store_sem.at[w])

    for w in range(count):
        load(w).start()
    for w in range(count):
        load(w).wait()
        store(w).start()
    for w in range(count):
        store(w).wait()


def pack_columns(tile, slots, part, parts):
    rows = tile.shape[0] // parts
    count = slots.shape[0]
    any_space = pl.BlockSpec(memory_space=pl.ANY)
    return pl.pallas_call(
        functools.partial(pack_kernel, part),
        out_shape=jax.ShapeDtypeStruct((count, rows, NB), tile.dtype),
        in_specs=[pl.BlockSpec(memory_space=pltpu.SMEM), any_space],
        out_specs=any_space,
        scratch_shapes=[
            pltpu.VMEM((count, rows, NB), tile.dtype),
            pltpu.SemaphoreType.DMA((count,)),
            pltpu.SemaphoreType.DMA((count,)),
        ],
        cost_estimate=pl.CostEstimate(
            flops=0, transcendentals=0, bytes_accessed=8 * count * rows * NB
        ),
        name="pack_columns",
    )(slots, tile)


def column_kernel(slots, ghosts, heads, tile_ref, ghost_ref, factor_ref, out_ref, held):
    out_ref[...] = tile_ref[...]
    held[...] = ghost_ref[...]

    def step(w, carry):
        at = pl.multiple_of(slots[w] * NB, NB)
        ghost = ghosts[w]
        head = heads[w]
        own_rows = pl.multiple_of((1 - head) * NB, NB)
        other_rows = pl.multiple_of(head * NB, NB)
        window = jnp.concatenate([out_ref[:, pl.ds(at, NB)], held[ghost]], axis=1)
        factor = jnp.concatenate(
            [factor_ref[w, pl.ds(own_rows, NB), :], factor_ref[w, pl.ds(other_rows, NB), :]], axis=0
        )
        turned = product(window, factor, ((1,), (0,)))
        first, second = turned[:, :NB], turned[:, NB:]
        is_head = head == 1
        out_ref[:, pl.ds(at, NB)] = jnp.where(is_head, first, second)
        held[ghost] = jnp.where(is_head, second, first)
        return carry

    lax.fori_loop(0, factor_ref.shape[0], step, 0)


def turn_columns(tile, ghost, factors, slots, ghosts, heads, part):
    width = tile.shape[1]
    count, rows, _ = ghost.shape
    order = factors.shape[-1]
    return pl.pallas_call(
        column_kernel,
        out_shape=jax.ShapeDtypeStruct((rows, width), tile.dtype),
        grid_spec=pltpu.PrefetchScalarGridSpec(
            num_scalar_prefetch=3,
            grid=(1,),
            in_specs=[
                pl.BlockSpec((rows, width), lambda i, *_: (part, 0)),
                pl.BlockSpec((count, rows, NB), lambda i, *_: (0, 0, 0)),
                pl.BlockSpec((count, order, order), lambda i, *_: (0, 0, 0)),
            ],
            out_specs=pl.BlockSpec((rows, width), lambda i, *_: (0, 0)),
            scratch_shapes=[pltpu.VMEM((count, rows, NB), tile.dtype)],
        ),
        compiler_params=pltpu.CompilerParams(vmem_limit_bytes=VMEM_LIMIT),
        cost_estimate=pl.CostEstimate(
            flops=6 * count * rows * order * order,
            transcendentals=0,
            bytes_accessed=4 * (2 * rows * width + count * rows * NB + count * order * order),
        ),
        name="turn_columns",
    )(slots, ghosts, heads, tile, ghost, factors)


def exchange_columns(tile, blocks, parts):
    position = lax.axis_index("cols")
    heads = (blocks % 2 == position).astype(jnp.int32)
    own = blocks + 1 - heads
    other = blocks + heads
    slots = own // 2
    same = other[:, None] == other[None, :]
    ghosts = jnp.argmax(same, axis=1).astype(jnp.int32)
    packed, came = [], []
    for part in range(parts):
        packed.append(pack_columns(tile, slots, part, parts))
        came.append(lax.ppermute(packed[part], "cols", [(0, 1), (1, 0)]))
    return packed, came, (slots, ghosts, heads)


def from_behind(value, axis, steps):
    count = lax.axis_size(axis)
    pairs = [(source, (source + steps) % count) for source in range(count)]
    return lax.ppermute(value, axis, pairs)


def columns_of_many(tile, blocks, whole_factors, chains):
    position = lax.axis_index("cols")
    devices = lax.axis_size("cols")

    def owned(ids):
        parts, places = [], []
        for block in ids:
            start = block // devices * NB
            mine = block % devices == position
            part = lax.dynamic_slice_in_dim(tile, start, NB, 1)
            parts.append(jnp.where(mine, part, jnp.zeros_like(part)))
            places.append((start, mine))
        return jnp.stack(parts), places

    for first in range(0, blocks.shape[0], chains):
        ids = [blocks[first + c] for c in range(chains)]
        left, left_places = owned(ids)
        right, right_places = owned([block + 1 for block in ids])
        window = jnp.concatenate(
            [left + from_behind(left, "cols", 1), right + from_behind(right, "cols", -1)], axis=2
        )
        turned = jnp.einsum(
            "crj,cji->cri",
            window,
            whole_factors[first : first + chains],
            precision=lax.Precision.HIGHEST,
            preferred_element_type=jnp.float32,
        )
        for c in range(chains):
            for (start, mine), new in (
                (left_places[c], turned[c, :, :NB]),
                (right_places[c], turned[c, :, NB:]),
            ):
                now = lax.dynamic_slice_in_dim(tile, start, NB, 1)
                tile = lax.dynamic_update_slice_in_dim(tile, jnp.where(mine, new, now), start, 1)
    return tile


def plan_kernel(devices, slots, count, blocks, me_ref, plan):
    me = me_ref[0]

    def clear(t, carry):
        for row in range(slots + 1):
            plan[row, t] = -1
        for row in range(slots + 1, slots + 4):
            plan[row, t] = 0
        return carry

    lax.fori_loop(0, count, clear, 0)
    block = [blocks[w] for w in range(count)]
    owner = [lax.rem(b, devices) for b in block]
    when = []
    for w in range(count):
        odd = lax.rem(owner[w], 2)
        step = odd
        for v in range(w):
            clash = (
                (block[w] == block[v])
                | (block[w] == block[v] + 1)
                | (block[w] + 1 == block[v])
                | ((owner[w] == owner[v]) & (odd == 1))
            )
            step = jnp.maximum(step, jnp.where(clash, when[v] + 1, 0))
        when.append(step)
        kind = jnp.where(odd == 0, 1, jnp.where(lax.rem(owner[w], 4) == 1, 2, 4))
        plan[slots + 2, step] = plan[slots + 2, step] | kind
        plan[slots + 3, 0] = jnp.maximum(plan[slots + 3, 0], step + 1)
        is_head = owner[w] == me

        @pl.when(is_head | (lax.rem(owner[w] + 1, devices) == me))
        def _():
            slot = jnp.where(is_head, block[w], block[w] + 1) // devices
            row = jnp.where(odd == 1, slots, slot)
            plan[row, step] = 2 * w + is_head.astype(jnp.int32)
            plan[slots + 1, step] = jnp.where(odd == 1, slot, plan[slots + 1, step])


def make_plan(blocks, me, devices, slots):
    count = blocks.shape[0]
    smem = pl.BlockSpec(memory_space=pltpu.SMEM)
    return pl.pallas_call(
        functools.partial(plan_kernel, devices, slots, count),
        out_shape=jax.ShapeDtypeStruct((slots + 4, count), jnp.int32),
        in_specs=[smem, smem],
        out_specs=smem,
        name="plan_steps",
    )(blocks, me.reshape(1))


def turn_block(code, job, mine, ghost, factor, pieces, chunk):
    head = lax.rem(code, 2)
    near = pl.multiple_of((1 - head) * NB, NB)
    far = pl.multiple_of(head * NB, NB)
    turn = jnp.concatenate(
        [
            factor[job, pl.ds(near, NB), pl.ds(near, NB)],
            factor[job, pl.ds(far, NB), pl.ds(near, NB)],
        ],
        axis=0,
    ).T

    def piece(j, carry):
        at = pl.ds(pl.multiple_of(j * chunk, NB), chunk)
        window = jnp.concatenate([mine[job, :, at], ghost[job, :, at]], axis=0)
        mine[job, :, at] = product(turn, window, ((1,), (0,)))
        return carry

    lax.fori_loop(0, pieces, piece, 0)


def row_kernel(
    slots, pieces, plan, t_ref, tile, even, odd, factors, out,
    mine, ghost, factor, mine_sem, ghost_sem, factor_sem, out_sem,
):
    t = t_ref[0]
    width = mine.shape[2]
    chunk = width // pieces
    jobs = slots + 1

    def place(job):
        slot = job if job < slots else plan[slots + 1, t]
        return pl.ds(pl.multiple_of(slot * NB, NB), NB)

    def loads(job):
        code = jnp.maximum(plan[job, t], 0)
        source = even.at[pl.ds(job * NB, NB), :] if job < slots else odd
        return (
            pltpu.make_async_copy(tile.at[place(job), :], mine.at[job], mine_sem.at[job]),
            pltpu.make_async_copy(source, ghost.at[job], ghost_sem.at[job]),
            pltpu.make_async_copy(factors.at[code // 2], factor.at[job], factor_sem.at[job]),
        )

    def store(job):
        return pltpu.make_async_copy(mine.at[job], out.at[place(job), :], out_sem.at[job])

    for job in range(jobs):

        @pl.when(plan[job, t] >= 0)
        def _():
            for copy in loads(job):
                copy.start()

    for job in range(jobs):

        @pl.when(plan[job, t] >= 0)
        def _():
            for copy in loads(job):
                copy.wait()
            turn_block(plan[job, t], job, mine, ghost, factor, pieces, chunk)
            store(job).start()

    for job in range(jobs):

        @pl.when(plan[job, t] >= 0)
        def _():
            store(job).wait()


def turn_rows(plan, t, tile, even, odd, factors):
    width = tile.shape[1]
    slots = tile.shape[0] // NB
    jobs = slots + 1
    order = factors.shape[-1]
    pieces = 4 if width % (4 * NB) == 0 else 1
    smem = pl.BlockSpec(memory_space=pltpu.SMEM)
    any_space = pl.BlockSpec(memory_space=pl.ANY)
    return pl.pallas_call(
        functools.partial(row_kernel, slots, pieces),
        out_shape=jax.ShapeDtypeStruct(tile.shape, tile.dtype),
        in_specs=[smem, smem] + [any_space] * 4,
        out_specs=any_space,
        scratch_shapes=[
            pltpu.VMEM((jobs, NB, width), tile.dtype),
            pltpu.VMEM((jobs, NB, width), tile.dtype),
            pltpu.VMEM((jobs, order, order), tile.dtype),
        ]
        + [pltpu.SemaphoreType.DMA((jobs,))] * 4,
        input_output_aliases={2: 0},
        compiler_params=pltpu.CompilerParams(vmem_limit_bytes=VMEM_LIMIT),
        name="turn_rows",
    )(plan, t.reshape(1), tile, even, odd, factors)


def even_kernel(base, pieces, plan, part, even, factors, *rest):
    out, mine, ghost, factor, mine_sem, ghost_sem, factor_sem, out_sem = rest[-8:]
    jobs, _, width = mine.shape
    chunk = width // pieces

    def load(job):
        return pltpu.make_async_copy(
            part.at[pl.ds(job * NB, NB), :], mine.at[job], mine_sem.at[job]
        )

    def others(job):
        code = jnp.maximum(plan[base + job, 0], 0)
        return (
            pltpu.make_async_copy(
                even.at[pl.ds(job * NB, NB), :], ghost.at[job], ghost_sem.at[job]
            ),
            pltpu.make_async_copy(factors.at[code // 2], factor.at[job], factor_sem.at[job]),
        )

    def store(job):
        return pltpu.make_async_copy(
            mine.at[job], out.at[pl.ds((base + job) * NB, NB), :], out_sem.at[job]
        )

    for job in range(jobs):
        load(job).start()

        @pl.when(plan[base + job, 0] >= 0)
        def _():
            for copy in others(job):
                copy.start()

    for job in range(jobs):
        load(job).wait()

        @pl.when(plan[base + job, 0] >= 0)
        def _():
            for copy in others(job):
                copy.wait()
            turn_block(plan[base + job, 0], job, mine, ghost, factor, pieces, chunk)

        store(job).start()
    for job in range(jobs):
        store(job).wait()


def turn_even(plan, part, even, factors, base, slots, tile=None):
    rows, width = part.shape
    jobs = rows // NB
    order = factors.shape[-1]
    pieces = 4 if width % (4 * NB) == 0 else 1
    any_space = pl.BlockSpec(memory_space=pl.ANY)
    extra = () if tile is None else (tile,)
    return pl.pallas_call(
        functools.partial(even_kernel, base, pieces),
        out_shape=jax.ShapeDtypeStruct((slots * NB, width), part.dtype),
        in_specs=[pl.BlockSpec(memory_space=pltpu.SMEM)] + [any_space] * (3 + len(extra)),
        out_specs=any_space,
        scratch_shapes=[
            pltpu.VMEM((jobs, NB, width), part.dtype),
            pltpu.VMEM((jobs, NB, width), part.dtype),
            pltpu.VMEM((jobs, order, order), part.dtype),
        ]
        + [pltpu.SemaphoreType.DMA((jobs,))] * 4,
        input_output_aliases={} if tile is None else {4: 0},
        compiler_params=pltpu.CompilerParams(vmem_limit_bytes=VMEM_LIMIT),
        cost_estimate=pl.CostEstimate(
            flops=6 * rows * 2 * NB * width, transcendentals=0, bytes_accessed=12 * rows * width
        ),
        name="turn_even",
    )(plan, part, even, factors, *extra)


def unset(shape, dtype):
    return pl.pallas_call(
        lambda out: None,
        out_shape=jax.ShapeDtypeStruct(shape, dtype),
        out_specs=pl.BlockSpec(memory_space=pl.ANY),
        name="unset",
    )()


def turn_all_rows(plan, column_parts, slots, whole_factors):
    devices = lax.axis_size("rows")

    def pairs(lows):
        ways = []
        for low in lows:
            high = (low + 1) % devices
            ways += [(low, high), (high, low)]
        return ways

    even_ways = pairs(range(0, devices, 2))
    odd_ways = {
        2: pairs(range(1, devices, 4)),
        4: pairs(range(3, devices, 4)),
        6: pairs(range(1, devices, 2)),
    }

    tile = None
    base = 0
    for column_part in column_parts:
        part, tile = column_part(tile)
        even = lax.ppermute(part, "rows", even_ways)
        tile = turn_even(plan, part, even, whole_factors, base, slots, tile)
        base += part.shape[0] // NB

    def exchange(kinds, tile, odd):
        even = unset(tile.shape, tile.dtype)
        far = unset(odd.shape, odd.dtype)
        if kinds & 1:
            even = lax.ppermute(tile, "rows", even_ways)
        if kinds & 6:
            far = lax.ppermute(odd, "rows", odd_ways[kinds & 6])
        return even, far

    branches = [functools.partial(exchange, kinds) for kinds in range(8)]

    def step(t, tile):
        odd = lax.dynamic_slice_in_dim(tile, plan[slots + 1, t] * NB, NB, 0)
        even, odd = lax.switch(plan[slots + 2, t], branches, tile, odd)
        return turn_rows(plan, t, tile, even, odd, whole_factors)

    return lax.fori_loop(1, plan[slots + 3, 0], step, tile)


def gather(factors, windows):
    if lax.axis_size("cols") == 2:
        other = lax.ppermute(factors, "cols", [(0, 1), (1, 0)])
        first = lax.axis_index("cols") == 0
        whole = jnp.concatenate(
            [jnp.where(first, factors, other), jnp.where(first, other, factors)], axis=3
        )
    else:
        whole = lax.all_gather(factors, "cols", axis=3, tiled=True)
    whole = lax.all_gather(whole, "rows", axis=2, tiled=True)
    return whole.reshape((windows,) + whole.shape[2:])


def local(matrix, starts, factors):
    advances, chains = starts.shape
    windows = advances * chains
    blocks = (starts // NB).reshape(windows)
    slots = matrix.shape[0] // NB
    parts = 2 if slots % 2 == 0 else 1
    plan = make_plan(blocks, lax.axis_index("rows"), lax.axis_size("rows"), slots)
    if lax.axis_size("cols") == 2:
        whole = gather(factors, windows)
        packed, came, tables = exchange_columns(matrix, blocks, parts)
        whole, plan, *_ = lax.optimization_barrier((whole, plan, *packed[1:]))

        def column_part(part, tile):
            ghost = came[part]
            if tile is not None:
                ghost, tile = lax.optimization_barrier((ghost, tile))
            return turn_columns(matrix, ghost, whole, *tables, part), tile

        column_parts = [functools.partial(column_part, part) for part in range(parts)]
    else:
        whole = gather(factors, windows)
        tile = columns_of_many(matrix, blocks, whole, chains)
        column_parts = [
            functools.partial(lambda piece, tile: (piece, tile), piece)
            for piece in jnp.split(tile, parts)
        ]
    return turn_all_rows(plan, column_parts, slots, whole)


def solution(mesh):
    return jax.shard_map(
        local,
        mesh=mesh,
        in_specs=(P("rows", "cols"), P(), P(None, None, "rows", "cols")),
        out_specs=P("rows", "cols"),
        check_vma=False,
    )
```
